32 devices in a mesh: rep: 2 (over x), grp: 2 (over core), ep: 8 (over z, y).
Axes of the slice: x: 2, y: 2, z: 4, core: 2. Of those that a mesh axis runs over, the one named last changes fastest.
Arguments:
- tokens: bfloat16 [4096, 2048], P(('rep', 'grp', 'ep')), parts along dimension 0, may hold values from -6 to 6
- routes: int32 [4096, 8], P(('rep', 'grp', 'ep')), parts along dimension 0, may hold values from 0 to 15, all different within a row; in each aligned block of 128 rows (0 to 127, 128 to 255, ...) at most 96 rows name the same one
- gates: float32 [4096, 8], P(('rep', 'grp', 'ep')), parts along dimension 0, may hold values from 0.1 to 1
- w_gate: bfloat16 [16, 2048, 768], P(('grp', 'ep')), may hold values from -0.125 to 0.125
- w_up: bfloat16 [16, 2048, 768], P(('grp', 'ep')), may hold values from -0.125 to 0.125
- w_down: bfloat16 [16, 768, 2048], P(('grp', 'ep')), may hold values from -0.21875 to 0.21875
Outputs:
- mixed: bfloat16 [4096, 2048], P(('rep', 'grp', 'ep')), parts along dimension 0
The draws below stay inside these ranges and needn't reach their ends.
There are 2 independent parts, one for each index of `rep`. The reference program is written for one: setup_inputs(seed, part) draws one part's arguments, and reference() takes and returns one part's arrays. A program takes and returns all parts, laid end to end along the dimension named above; an argument that names none is the same for every part. Nothing has to cross between parts.
Inputs may be any that keep to these rules, and one draw needn't show every extreme that they name: `routes`: each row names 8 different experts; within the rows of one device no expert is named by more than 96 rows, a bound that some block reaches.
All inputs are finite; a program needn't handle non-finite values.
Results may differ from the reference program's by a relative error of at most 0.0057.
Values may be sent and summed in bfloat16 or wider, within the bound.
A program may use at most 128 MiB of HBM per device.

```python
import math
import jax
import jax.numpy as jnp
import numpy as np
from jax import lax

D = 2048
H = 768
TOP = 8
TOK_DEV = 128
EXPERTS = 16
TOKENS = 2048
CAP = 96


def block_scale(key, extent, shards, least, largest):
    def one(axis_at, shards_of):
        steps = jax.random.uniform(jax.random.fold_in(jax.random.fold_in(key, 6), axis_at), (shards_of,), jnp.float32, least / len(shards), largest / len(shards))
        return jnp.repeat(jnp.exp(steps), extent[axis_at] // shards_of).reshape((-1,) + (1,) * (len(extent) - axis_at - 1))

    loudness = one(*shards[0])
    for cut in shards[1:]:
        loudness = loudness * one(*cut)
    return loudness


def routed_block(rng, own, number, rows, amount, top, limit, slope):
    sequence = jax.random.permutation(rng, amount)
    packed, usual = shares(amount, rows * top, limit, slope, True), shares(amount, rows * top, limit, slope, False)
    places = jnp.arange(amount)

    def named(sizes, turn):
        used = int((sizes > 0).sum())
        fixed = max(1, used // 4)
        shifted = fixed + (places - fixed + turn * (used - fixed)) % max(1, amount - fixed)
        return jnp.zeros((amount,), jnp.int32).at[sequence[jnp.where(places < fixed, places, shifted)]].set(jnp.asarray(sizes, jnp.int32))

    sizes = jnp.where(number % 4 == 0, named(packed, number // 4), named(usual, number - number // 4 - 1))
    mixed = jax.random.permutation(jax.random.fold_in(own, 3), amount)
    donor, taker = mixed[0:amount // 2 * 2:2], mixed[1:amount // 2 * 2:2]
    room = jnp.minimum(sizes[donor] - 1, limit - sizes[taker]) // 2
    room = jnp.where((donor == sequence[0]) | (taker == sequence[0]) | (sizes[taker] == 0), 0, jnp.maximum(room, 0))
    shifted = jax.random.randint(jax.random.fold_in(own, 4), (amount // 2,), 0, 1 << 20) % (room + 1)
    sizes = sizes.at[donor].add(-shifted).at[taker].add(shifted)
    items = jnp.searchsorted(jnp.cumsum(sizes), jnp.arange(rows * top), side="right").astype(jnp.int32)
    table = items.reshape(top, rows).T
    table = table[jax.random.permutation(jax.random.fold_in(own, 1), rows)]
    turn = jax.random.randint(jax.random.fold_in(own, 2), (rows, 1), 0, top)
    return jnp.take_along_axis(table, (jnp.arange(top)[None, :] + turn) % top, axis=1)


def shares(count, total, limit, lean, full):
    loads = [(1 << 20) // math.isqrt(grade ** lean) + 1 for grade in range(1, count + 1)]
    largest = limit if full else min(limit, max(-(-total // count), total * loads[0] // sum(loads)))
    least = 1 if total - largest >= count - 1 else 0
    holding, spare = [largest] + [least] * (count - 1), total - largest - least * (count - 1)
    while spare > 0:
        free = [i for i in range(1, count) if holding[i] < largest] or [i for i in range(1, count) if holding[i] < limit]
        pool, left = sum([loads[i] for i in free]), spare
        for i in free:
            more = min(limit - holding[i], max(1, left * loads[i] // pool), spare)
            holding[i] = holding[i] + more
            spare = spare - more
    return np.array(holding)


def normal_values(own_key, extent, width, most, shards=(), kind=jnp.bfloat16):
    level = block_scale(own_key, extent, shards, -0.22, 0.18) if shards else 1.0
    values = jax.random.normal(own_key, extent, jnp.float32) * width * level
    return jnp.minimum(jnp.maximum(values, -most), most).astype(kind)


def setup_inputs(seed: int = 0, part: int = 0) -> dict:
    keys = jax.random.split(jax.random.key(seed), 7)
    part_keys = jax.random.split(jax.random.fold_in(keys[6], part), 7)
    tokens = normal_values(part_keys[0], (TOKENS, D), 1.0, 6.0, ((0, 16),))
    routes_keys = jax.random.split(jax.random.fold_in(part_keys[1], 1), TOKENS // TOK_DEV)
    routes_turns = jax.random.permutation(jax.random.fold_in(part_keys[1], 3), TOKENS // TOK_DEV)
    routes = jax.vmap(lambda own, number: routed_block(jax.random.fold_in(part_keys[1], 2), own, number, TOK_DEV, EXPERTS, TOP, CAP, 2))(routes_keys, routes_turns).reshape((TOKENS, TOP))
    gates = jnp.clip(jnp.exp(math.log(1.0) - 2.3025851 * jax.random.uniform(part_keys[2], (TOKENS, TOP), jnp.float32) ** block_scale(part_keys[2], (TOKENS, TOP), ((0, 16),), -0.2, 0.2)), 0.1, 1.0)
    w_gate = normal_values(keys[3], (EXPERTS, D, H), D ** -0.5, 0.125, ((0, 16),))
    w_up = normal_values(keys[4], (EXPERTS, D, H), D ** -0.5, 0.125, ((0, 16),))
    w_down = normal_values(keys[5], (EXPERTS, H, D), H ** -0.5, 0.21875, ((0, 16),))
    return dict(tokens=tokens, routes=routes, gates=gates, w_gate=w_gate, w_up=w_up, w_down=w_down)


def reference(tokens, routes, gates, w_gate, w_up, w_down):
    sources = TOKENS // TOK_DEV
    block_ids = routes.reshape(sources, TOK_DEV * TOP)
    onehot = (block_ids[:, :, None] == jnp.arange(EXPERTS, dtype=jnp.int32)[None, None, :]).astype(jnp.int32)
    ranks = jnp.cumsum(onehot, axis=1) - 1
    slot = jnp.sum(ranks * onehot, axis=2).reshape(-1)
    flat_ids = routes.reshape(-1)
    source = (jnp.arange(TOKENS * TOP, dtype=jnp.int32) // (TOK_DEV * TOP)).astype(jnp.int32)
    position = flat_ids * (sources * CAP) + source * CAP + slot
    table = jnp.full((EXPERTS * sources * CAP,), TOKENS * TOP, jnp.int32)
    table = table.at[position].set(jnp.arange(TOKENS * TOP, dtype=jnp.int32)).reshape(EXPERTS, sources * CAP)
    padded_tokens = jnp.concatenate([tokens, jnp.zeros((1, D), tokens.dtype)], axis=0)
    padded_gates = jnp.concatenate([gates.reshape(-1), jnp.zeros((1,), jnp.float32)], axis=0)

    def one_expert(total, inputs):
        entries, wg, wu, wd = inputs
        token_idx = (entries // TOP).astype(jnp.int32)
        rows = padded_tokens[token_idx]
        gate_act = jnp.dot(rows, wg, preferred_element_type=jnp.float32)
        up_act = jnp.dot(rows, wu, preferred_element_type=jnp.float32)
        hidden = (jax.nn.silu(gate_act) * up_act).astype(jnp.bfloat16)
        result = jnp.dot(hidden, wd, preferred_element_type=jnp.float32).astype(jnp.bfloat16)
        weighted = padded_gates[entries][:, None] * result.astype(jnp.float32)
        return total.at[token_idx].add(weighted), None

    start = jnp.zeros((TOKENS + 1, D), jnp.float32)
    total, unused = lax.scan(one_expert, start, (table, w_gate, w_up, w_down))
    return total[:TOKENS].astype(jnp.bfloat16)
```

```python
import jax
import jax.numpy as jnp
from jax import lax
from jax.sharding import PartitionSpec as P


def expert_rows(rows, w_gate, w_up, w_down):
    gate_act = jnp.dot(rows, w_gate[0], preferred_element_type=jnp.float32)
    up_act = jnp.dot(rows, w_up[0], preferred_element_type=jnp.float32)
    hidden = (jax.nn.silu(gate_act) * up_act).astype(jnp.bfloat16)
    return jnp.dot(hidden, w_down[0], preferred_element_type=jnp.float32).astype(jnp.bfloat16)


def routed(tokens, routes, gates, w_gate, w_up, w_down):
    tok_rows, width = tokens.shape
    top = routes.shape[1]
    groups = lax.axis_size("grp")
    members = lax.axis_size("ep")
    experts = groups * members
    capacity = tok_rows * top * 3 // (2 * experts)
    flat_ids = routes.reshape(-1)
    onehot = (flat_ids[:, None] == jnp.arange(experts, dtype=jnp.int32)[None, :]).astype(jnp.int32)
    ranks = jnp.cumsum(onehot, axis=0) - 1
    slot = jnp.sum(ranks * onehot, axis=1)
    position = flat_ids * capacity + slot
    token_idx = jnp.arange(tok_rows * top, dtype=jnp.int32) // top
    send = jnp.zeros((experts * capacity, width), jnp.bfloat16).at[position].set(tokens[token_idx])
    sectioned = send.reshape(groups, members, capacity, width)
    arrived = lax.all_to_all(
        lax.all_to_all(sectioned, "grp", split_axis=0, concat_axis=0, tiled=True),
        "ep",
        split_axis=1,
        concat_axis=1,
        tiled=True,
    )
    results = expert_rows(arrived.reshape(-1, width), w_gate, w_up, w_down)
    results = results.reshape(groups, members, capacity, width)
    back = lax.all_to_all(
        lax.all_to_all(results, "grp", split_axis=0, concat_axis=0, tiled=True),
        "ep",
        split_axis=1,
        concat_axis=1,
        tiled=True,
    )
    picked = back.reshape(experts * capacity, width)[position].astype(jnp.float32)
    picked = picked.reshape(tok_rows, top, width)
    mixed = jnp.sum(picked * gates[:, :, None], axis=1)
    return mixed.astype(jnp.bfloat16)


def gathered(tokens, routes, gates, w_gate, w_up, w_down):
    axes = ("grp", "ep")
    experts = lax.axis_size("grp") * lax.axis_size("ep")
    me = lax.axis_index("grp") * lax.axis_size("ep") + lax.axis_index("ep")
    ids = jnp.arange(experts, dtype=jnp.int32)
    share = jnp.sum(jnp.where(routes[:, :, None] == ids, gates[:, :, None], 0.0), axis=1)
    shares = lax.all_gather(share, axes, axis=0, tiled=True)
    mine = jnp.sum(jnp.where(ids == me, shares, 0.0), axis=1, keepdims=True)
    rows = lax.all_gather(tokens, axes, axis=0, tiled=True)
    gate_act = jnp.dot(rows, w_gate[0], preferred_element_type=jnp.float32)
    up_act = jnp.dot(rows, w_up[0], preferred_element_type=jnp.float32)
    hidden = (jax.nn.silu(gate_act) * up_act).astype(jnp.bfloat16)
    out = jnp.dot(hidden, w_down[0], preferred_element_type=jnp.float32)
    part = (out * mine).astype(jnp.bfloat16)
    return lax.psum_scatter(part, axes, scatter_dimension=0, tiled=True)


def solution(mesh):
    experts = mesh.shape["grp"] * mesh.shape["ep"]

    def local(tokens, routes, gates, w_gate, w_up, w_down):
        dense = routes.shape[1] * 3 >= experts
        body = gathered if dense else routed
        return body(tokens, routes, gates, w_gate, w_up, w_down)

    return jax.shard_map(
        local,
        mesh=mesh,
        in_specs=(
            P(("rep", "grp", "ep"), None),
            P(("rep", "grp", "ep"), None),
            P(("rep", "grp", "ep"), None),
            P(("grp", "ep"), None, None),
            P(("grp", "ep"), None, None),
            P(("grp", "ep"), None, None),
        ),
        out_specs=P(("rep", "grp", "ep"), None),
        check_vma=False,
    )
```

```python
import jax
import jax.numpy as jnp
from jax import lax
from jax.experimental import pallas as pl
from jax.experimental.pallas import tpu as pltpu
from jax.sharding import PartitionSpec as P

B_SHARE = 4


def expert_rows(rows, w_gate, w_up, w_down):
    gate_act = jnp.dot(rows, w_gate[0], preferred_element_type=jnp.float32)
    up_act = jnp.dot(rows, w_up[0], preferred_element_type=jnp.float32)
    hidden = (jax.nn.silu(gate_act) * up_act).astype(jnp.bfloat16)
    return jnp.dot(hidden, w_down[0], preferred_element_type=jnp.float32).astype(jnp.bfloat16)


def routed(tokens, routes, gates, w_gate, w_up, w_down):
    tok_rows, width = tokens.shape
    top = routes.shape[1]
    groups = lax.axis_size("grp")
    members = lax.axis_size("ep")
    experts = groups * members
    capacity = tok_rows * top * 3 // (2 * experts)
    flat_ids = routes.reshape(-1)
    onehot = (flat_ids[:, None] == jnp.arange(experts, dtype=jnp.int32)[None, :]).astype(jnp.int32)
    ranks = jnp.cumsum(onehot, axis=0) - 1
    slot = jnp.sum(ranks * onehot, axis=1)
    position = flat_ids * capacity + slot
    token_idx = jnp.arange(tok_rows * top, dtype=jnp.int32) // top
    send = jnp.zeros((experts * capacity, width), jnp.bfloat16).at[position].set(tokens[token_idx])
    sectioned = send.reshape(groups, members, capacity, width)
    arrived = lax.all_to_all(
        lax.all_to_all(sectioned, "grp", split_axis=0, concat_axis=0, tiled=True),
        "ep",
        split_axis=1,
        concat_axis=1,
        tiled=True,
    )
    results = expert_rows(arrived.reshape(-1, width), w_gate, w_up, w_down)
    results = results.reshape(groups, members, capacity, width)
    back = lax.all_to_all(
        lax.all_to_all(results, "grp", split_axis=0, concat_axis=0, tiled=True),
        "ep",
        split_axis=1,
        concat_axis=1,
        tiled=True,
    )
    picked = back.reshape(experts * capacity, width)[position].astype(jnp.float32)
    picked = picked.reshape(tok_rows, top, width)
    mixed = jnp.sum(picked * gates[:, :, None], axis=1)
    return mixed.astype(jnp.bfloat16)


def mixing_kernel(tokens_ref, shares_ref, wg_hbm, wu_hbm, wd_hbm, out_ref,
                  xbuf, sbuf, wg, wu, wd, hid, scale, own, ysend, yrecv, zsend, zrecv, bsend, brecv,
                  s_load, s_wsend, s_wrecv, s_ssend, s_srecv,
                  s_zs1, s_zs2, s_zr1, s_zr2, s_yas, s_yar, s_ybs, s_ybr,
                  s_pys, s_pyr, s_pzs, s_pzr, s_pbs, s_pbr):
    rows = tokens_ref.shape[0]
    row_b = brecv.shape[1]
    row_a = rows - row_b
    kept = row_a + 2 * row_b
    hidden = wg.shape[2]
    chunks, _, wide = bsend.shape
    planes = xbuf.shape[0]
    last = planes - 1
    members = 2 * planes
    me = lax.axis_index("ep")
    core = lax.axis_index("grp")
    z, y = me // 2, me % 2
    twin = {"grp": 1 - core}
    across = {"ep": z * 2 + (1 - y)}
    end = (z == 0) | (z == last)
    inner = jnp.logical_not(end)
    low = z < planes // 2

    def remote(src, dst, send, recv, to):
        return pltpu.make_async_remote_copy(src_ref=src, dst_ref=dst, send_sem=send, recv_sem=recv, device_id=to,
                                            device_id_type=pl.DeviceIdType.MESH)

    barrier = pltpu.get_barrier_semaphore()
    pl.semaphore_signal(barrier, inc=1, device_id=twin, device_id_type=pl.DeviceIdType.MESH)
    for k in range(1, members):
        pl.semaphore_signal(barrier, inc=1, device_id={"ep": lax.rem(me + k, members)}, device_id_type=pl.DeviceIdType.MESH)

    loads = [pltpu.make_async_copy(tokens_ref, xbuf.at[z, pl.ds(0, rows)], s_load.at[0]),
             pltpu.make_async_copy(wg_hbm.at[0], wg.at[0], s_load.at[1]),
             pltpu.make_async_copy(wu_hbm.at[0], wu.at[0], s_load.at[2]),
             pltpu.make_async_copy(wd_hbm.at[0], wd.at[pl.ds(0, hidden)], s_load.at[3])]
    for copy in loads:
        copy.start()
    pl.semaphore_wait(barrier, members)

    rng_a, rng_b = pl.ds(0, row_a), pl.ds(row_a, row_b)
    rng_ob, rng_oa = pl.ds(rows, row_b), pl.ds(rows + row_b, row_a)

    def hop1(p, slot, step, src):
        return remote(src, xbuf.at[p, pl.ds(0, rows)], s_zs1.at[slot], s_zr1.at[p], {"ep": (z + step) * 2 + y})

    def hop2(p, slot, step):
        return remote(xbuf.at[p, rng_ob], xbuf.at[p, rng_ob], s_zs2.at[slot], s_zr2.at[p], {"ep": (z + step) * 2 + y})

    def cross_a(p, src):
        return remote(src, xbuf.at[p, rng_oa], s_yas.at[p], s_yar.at[p], across)

    own_b = remote(tokens_ref.at[rng_b], xbuf.at[z, rng_ob], s_ybs.at[0], s_ybr.at[0], across)
    own_b.start()

    def both(make, act):
        pl.when(z < last)(lambda: act(make(z, 1)))
        pl.when(z > 0)(lambda: act(make(planes, -1)))

    first1 = lambda slot, step: hop1(z, slot, step, tokens_ref)
    first2 = lambda slot, step: hop2(z, slot, step)
    both(first1, lambda c: c.start())
    own_a = cross_a(z, tokens_ref.at[rng_a])
    own_a.start()

    def share_copy(k):
        to = lax.rem(me + k, members)
        return remote(shares_ref.at[to], sbuf.at[me], s_ssend.at[k], s_srecv.at[k], {"ep": to})

    for k in range(1, members):
        share_copy(k).start()
    sbuf[me] = shares_ref[me]
    weights = [remote(wg_hbm.at[0], wg.at[1], s_wsend.at[0], s_wrecv.at[0], twin),
               remote(wu_hbm.at[0], wu.at[1], s_wsend.at[1], s_wrecv.at[1], twin),
               remote(wd_hbm.at[0], wd.at[pl.ds(hidden, hidden)], s_wsend.at[2], s_wrecv.at[2], twin)]
    for copy in weights:
        copy.start()

    own_b.wait_recv()
    both(first2, lambda c: c.start())

    def order(s):
        if planes == 2:
            near = s
        else:
            near = jnp.where(end, s, jnp.where(s == 0, 1, jnp.where(s == 1, 0, s)))
        return jnp.where(low, near, last - near)

    def forward(p, act1, act2):
        pl.when((p < z) & (z < last))(lambda: act1(hop1(p, p, 1, xbuf.at[p, pl.ds(0, rows)]), hop2(p, p, 1)))
        pl.when((p > z) & (z > 0))(lambda: act1(hop1(p, p, -1, xbuf.at[p, pl.ds(0, rows)]), hop2(p, p, -1)))

    def relay(s):
        p = order(s)
        hop1(p, p, 0, xbuf.at[p, pl.ds(0, rows)]).wait_recv()
        forward(p, lambda a, b: a.start(), None)
        cross_a(p, xbuf.at[p, rng_a]).start()
        hop2(p, p, 0).wait_recv()
        forward(p, lambda a, b: b.start(), None)

    def column(src, e):
        line = sbuf[src, pl.ds(e, 1), :]
        diag = lax.broadcasted_iota(jnp.int32, (rows, rows), 0) == lax.broadcasted_iota(jnp.int32, (rows, rows), 1)
        return jnp.sum(jnp.where(diag, jnp.broadcast_to(line, (rows, rows)), 0.0), axis=1, keepdims=True)

    def arrived(p):
        cross_a(p, xbuf.at[p, rng_a]).wait_recv()
        for e in range(2):
            scale[e, pl.ds(0, rows), :] = jnp.broadcast_to(column(p * 2 + y, e), (rows, 128))
            other = jnp.broadcast_to(column(p * 2 + 1 - y, e), (rows, 128))
            scale[e, rng_ob, :] = other[row_a:]
            scale[e, rng_oa, :] = other[:row_a]

    tile = 256

    def make_hidden(p, e):
        @pl.loop(0, hidden // tile)
        def _(t):
            cols = pl.ds(pl.multiple_of(t * tile, tile), tile)
            x = xbuf[p]
            g = jnp.dot(x, wg[e, :, cols], preferred_element_type=jnp.float32)
            u = jnp.dot(x, wu[e, :, cols], preferred_element_type=jnp.float32)
            h = g / (1.0 + jnp.exp(-g)) * u * scale[e, :, pl.ds(0, 1)]
            hid[:, pl.ds(pl.multiple_of(e * hidden + t * tile, tile), tile)] = h.astype(jnp.bfloat16)

    def part_y(p, n):
        return remote(ysend.at[p, n], yrecv.at[p, n], s_pys.at[p, n], s_pyr.at[p, n], across)

    def make_down(p):
        @pl.loop(0, chunks)
        def _(n):
            acc = jnp.dot(hid[...], wd[:, pl.ds(pl.multiple_of(n * wide, wide), wide)], preferred_element_type=jnp.float32)
            ysend[p, n] = acc[kept:].astype(jnp.bfloat16)
            part_y(p, n).start()
            own[p, n] = acc[:kept]

    def part_z(p, n, step):
        slot = jnp.where((step < 0) & (z + step == p), planes, p)
        return remote(zsend.at[p, n], zrecv.at[slot, n], s_pzs.at[p, n], s_pzr.at[slot, n], {"ep": (z + step) * 2 + y})

    def from_z(slot, n):
        remote(zsend.at[0, n], zrecv.at[slot, n], s_pzs.at[0, n], s_pzr.at[slot, n], across).wait_recv()
        own_p = jnp.where(slot == planes, z, slot)
        own[own_p, n] = own[own_p, n] + zrecv[slot, n].astype(jnp.float32)

    def toward(p, act):
        pl.when(p < z)(lambda: act(-1))
        pl.when(p > z)(lambda: act(1))

    def add_y(p, n):
        part_y(p, n).wait_recv()
        own[p, n, pl.ds(0, row_a), :] = own[p, n, pl.ds(0, row_a), :] + yrecv[p, n].astype(jnp.float32)

    def reduce_on(p, n):
        add_y(p, n)

        @pl.when(inner)
        def _():
            from_z(p, n)

        zsend[p, n] = own[p, n].astype(jnp.bfloat16)
        toward(p, lambda step: part_z(p, n, step).start())

    for copy in loads:
        copy.wait()
    for k in range(1, members):
        share_copy(k).wait_recv()
    arrived(z)
    make_hidden(z, 0)
    relay(1)
    pl.when(inner)(lambda: relay(2))
    for copy in weights:
        copy.wait_recv()
    make_hidden(z, 1)
    make_down(z)

    @pl.loop(1, planes)
    def _(s):
        p = order(s)
        pl.when(((s == 2) & end) | (s == 3))(lambda: relay(s))
        arrived(p)
        pl.loop(0, 2)(lambda e: make_hidden(p, e))
        make_down(p)

        @pl.when(end)
        def _():
            pl.loop(0, chunks)(lambda n: reduce_on(p, n))

    @pl.when(inner)
    def _():
        near = jnp.where(low, 0, last)
        pl.loop(0, chunks)(lambda n: reduce_on(last - z, n))

        @pl.loop(0, chunks)
        def _(n):
            reduce_on(last - near, n)
            reduce_on(near, n)

    def part_b(n):
        return remote(bsend.at[n], brecv.at[n], s_pbs.at[n], s_pbr.at[n], across)

    @pl.loop(0, chunks)
    def _(n):
        add_y(z, n)
        pl.when(z > 0)(lambda: from_z(z, n))
        pl.when(z < last)(lambda: from_z(planes, n))
        bsend[n] = own[z, n, rng_ob, :].astype(jnp.bfloat16)
        part_b(n).start()

    for n in range(chunks):
        part_b(n).wait_recv()
        cols = pl.ds(n * wide, wide)
        out_ref[rng_a, cols] = own[z, n, rng_a, :].astype(jnp.bfloat16)
        out_ref[rng_b, cols] = (own[z, n, rng_b, :] + brecv[n].astype(jnp.float32)).astype(jnp.bfloat16)

    own_b.wait_send()
    both(first1, lambda c: c.wait_send())
    both(first2, lambda c: c.wait_send())
    for k in range(1, members):
        share_copy(k).wait_send()
    for copy in weights:
        copy.wait_send()

    def both_sent(a, b):
        a.wait_send()
        b.wait_send()

    @pl.loop(0, planes)
    def _(p):
        cross_a(p, xbuf.at[p, rng_a]).wait_send()
        forward(p, both_sent, None)

        @pl.loop(0, chunks)
        def _(n):
            part_y(p, n).wait_send()
            toward(p, lambda step: part_z(p, n, step).wait_send())

    for n in range(chunks):
        part_b(n).wait_send()


def fused(tokens, routes, gates, w_gate, w_up, w_down):
    rows, width = tokens.shape
    hidden = w_gate.shape[2]
    members = lax.axis_size("ep")
    planes = members // 2
    row_b = rows * B_SHARE // 8
    row_a = rows - row_b
    kept = row_a + 2 * row_b
    chunks = 4
    wide = width // chunks
    core = lax.axis_index("grp")
    ids = lax.rem(core + jnp.arange(8, dtype=jnp.int32), 2)[None, :] * members + jnp.arange(members, dtype=jnp.int32)[:, None]
    shares = jnp.sum(jnp.where(routes.T[:, None, None, :] == ids[None, :, :, None], gates.T[:, None, None, :], 0.0), axis=0)
    bf, dma = jnp.bfloat16, pltpu.SemaphoreType.DMA
    flops = 2 * members * rows * width * hidden * 6
    return pl.pallas_call(
        mixing_kernel,
        out_shape=jax.ShapeDtypeStruct((rows, width), bf),
        in_specs=[pl.BlockSpec(memory_space=pltpu.VMEM)] * 2 + [pl.BlockSpec(memory_space=pl.ANY)] * 3,
        out_specs=pl.BlockSpec(memory_space=pltpu.VMEM),
        scratch_shapes=[
            pltpu.VMEM((planes, 2 * rows, width), bf),
            pltpu.VMEM((members, 8, rows), jnp.float32),
            pltpu.VMEM((2, width, hidden), bf),
            pltpu.VMEM((2, width, hidden), bf),
            pltpu.VMEM((2 * hidden, width), bf),
            pltpu.VMEM((2 * rows, 2 * hidden), bf),
            pltpu.VMEM((2, 2 * rows, 128), jnp.float32),
            pltpu.VMEM((planes, chunks, kept, wide), jnp.float32),
            pltpu.VMEM((planes, chunks, row_a, wide), bf),
            pltpu.VMEM((planes, chunks, row_a, wide), bf),
            pltpu.VMEM((planes, chunks, kept, wide), bf),
            pltpu.VMEM((planes + 1, chunks, kept, wide), bf),
            pltpu.VMEM((chunks, row_b, wide), bf),
            pltpu.VMEM((chunks, row_b, wide), bf),
            dma((4,)), dma((3,)), dma((3,)), dma((members,)), dma((members,)),
            dma((planes + 1,)), dma((planes + 1,)), dma((planes,)), dma((planes,)),
            dma((planes,)), dma((planes,)), dma((1,)), dma((1,)),
            dma((planes, chunks)), dma((planes, chunks)), dma((planes, chunks)), dma((planes + 1, chunks)),
            dma((chunks,)), dma((chunks,)),
        ],
        compiler_params=pltpu.CompilerParams(collective_id=0, has_side_effects=True, vmem_limit_bytes=60 * 1024 * 1024),
        cost_estimate=pl.CostEstimate(flops=flops, bytes_accessed=20 * 1024 * 1024, transcendentals=0),
    )(tokens, shares, w_gate, w_up, w_down)


def solution(mesh):
    groups, members = mesh.shape["grp"], mesh.shape["ep"]

    def local(tokens, routes, gates, w_gate, w_up, w_down):
        dense = groups == 2 and members == 8 and routes.shape[1] * 3 >= groups * members
        body = fused if dense else routed
        return body(tokens, routes, gates, w_gate, w_up, w_down)

    return jax.shard_map(
        local,
        mesh=mesh,
        in_specs=(
            P(("rep", "grp", "ep"), None),
            P(("rep", "grp", "ep"), None),
            P(("rep", "grp", "ep"), None),
            P(("grp", "ep"), None, None),
            P(("grp", "ep"), None, None),
            P(("grp", "ep"), None, None),
        ),
        out_specs=P(("rep", "grp", "ep"), None),
        check_vma=False,
    )
```

```python
import jax
import jax.numpy as jnp
from jax import lax
from jax.experimental import pallas as pl
from jax.experimental.pallas import tpu as pltpu
from jax.sharding import PartitionSpec as P

B_SHARE = 4


def expert_rows(rows, w_gate, w_up, w_down):
    gate_act = jnp.dot(rows, w_gate[0], preferred_element_type=jnp.float32)
    up_act = jnp.dot(rows, w_up[0], preferred_element_type=jnp.float32)
    hidden = (jax.nn.silu(gate_act) * up_act).astype(jnp.bfloat16)
    return jnp.dot(hidden, w_down[0], preferred_element_type=jnp.float32).astype(jnp.bfloat16)


def routed(tokens, routes, gates, w_gate, w_up, w_down):
    tok_rows, width = tokens.shape
    top = routes.shape[1]
    groups = lax.axis_size("grp")
    members = lax.axis_size("ep")
    experts = groups * members
    capacity = tok_rows * top * 3 // (2 * experts)
    flat_ids = routes.reshape(-1)
    onehot = (flat_ids[:, None] == jnp.arange(experts, dtype=jnp.int32)[None, :]).astype(jnp.int32)
    ranks = jnp.cumsum(onehot, axis=0) - 1
    slot = jnp.sum(ranks * onehot, axis=1)
    position = flat_ids * capacity + slot
    token_idx = jnp.arange(tok_rows * top, dtype=jnp.int32) // top
    send = jnp.zeros((experts * capacity, width), jnp.bfloat16).at[position].set(tokens[token_idx])
    sectioned = send.reshape(groups, members, capacity, width)
    arrived = lax.all_to_all(
        lax.all_to_all(sectioned, "grp", split_axis=0, concat_axis=0, tiled=True),
        "ep",
        split_axis=1,
        concat_axis=1,
        tiled=True,
    )
    results = expert_rows(arrived.reshape(-1, width), w_gate, w_up, w_down)
    results = results.reshape(groups, members, capacity, width)
    back = lax.all_to_all(
        lax.all_to_all(results, "grp", split_axis=0, concat_axis=0, tiled=True),
        "ep",
        split_axis=1,
        concat_axis=1,
        tiled=True,
    )
    picked = back.reshape(experts * capacity, width)[position].astype(jnp.float32)
    picked = picked.reshape(tok_rows, top, width)
    mixed = jnp.sum(picked * gates[:, :, None], axis=1)
    return mixed.astype(jnp.bfloat16)


def mixing_kernel(tokens_ref, shares_ref, wg_hbm, wu_hbm, wd_hbm, out_ref,
                  xbuf, sbuf, wg, wu, wd, hid, scale, own, ysend, yrecv, zsend_a, zsend_b, zrecv_a, zrecv_b, bsend, brecv,
                  s_load, s_wsend, s_wrecv, s_ssend, s_srecv,
                  s_zs1, s_zs2, s_zr1, s_zr2, s_yas, s_yar, s_ybs, s_ybr,
                  s_pys, s_pyr, s_pzs_a, s_pzr_a, s_pzs_b, s_pzr_b, s_pbs, s_pbr):
    rows = tokens_ref.shape[0]
    row_b = brecv.shape[1]
    row_a = rows - row_b
    hidden = wg.shape[2]
    chunks, _, wide = bsend.shape
    planes = xbuf.shape[0]
    last = planes - 1
    members = 2 * planes
    me = lax.axis_index("ep")
    core = lax.axis_index("grp")
    z, y = me // 2, me % 2
    twin = {"grp": 1 - core}
    across = {"ep": z * 2 + (1 - y)}
    end = (z == 0) | (z == last)
    inner = jnp.logical_not(end)
    low = z < planes // 2

    def remote(src, dst, send, recv, to):
        return pltpu.make_async_remote_copy(src_ref=src, dst_ref=dst, send_sem=send, recv_sem=recv, device_id=to,
                                            device_id_type=pl.DeviceIdType.MESH)

    barrier = pltpu.get_barrier_semaphore()
    pl.semaphore_signal(barrier, inc=1, device_id=twin, device_id_type=pl.DeviceIdType.MESH)
    for k in range(1, members):
        pl.semaphore_signal(barrier, inc=1, device_id={"ep": lax.rem(me + k, members)}, device_id_type=pl.DeviceIdType.MESH)

    rng_a, rng_b = pl.ds(0, row_a), pl.ds(row_a, row_b)
    rng_oa, rng_mb = pl.ds(row_a, row_a), pl.ds(2 * row_a, row_b)
    rng_ob, rng_bb = pl.ds(2 * row_a + row_b, row_b), pl.ds(2 * row_a, 2 * row_b)
    rng_aa = pl.ds(0, 2 * row_a)
    own_bb = pl.ds(row_a, 2 * row_b)

    loads = [pltpu.make_async_copy(tokens_ref.at[rng_b], xbuf.at[z, rng_mb], s_load.at[0]),
             pltpu.make_async_copy(tokens_ref.at[rng_a], xbuf.at[z, rng_a], s_load.at[4]),
             pltpu.make_async_copy(wg_hbm.at[0], wg.at[0], s_load.at[1]),
             pltpu.make_async_copy(wu_hbm.at[0], wu.at[0], s_load.at[2]),
             pltpu.make_async_copy(wd_hbm.at[0], wd.at[pl.ds(0, hidden)], s_load.at[3])]
    for copy in loads:
        copy.start()
    pl.semaphore_wait(barrier, members)

    def hop1(p, slot, step, src):
        return remote(src, xbuf.at[p, rng_a], s_zs1.at[slot], s_zr1.at[p], {"ep": (z + step) * 2 + y})

    def hop2(p, slot, step):
        return remote(xbuf.at[p, rng_bb], xbuf.at[p, rng_bb], s_zs2.at[slot], s_zr2.at[p], {"ep": (z + step) * 2 + y})

    def cross_a(p, src):
        return remote(src, xbuf.at[p, rng_oa], s_yas.at[p], s_yar.at[p], across)

    own_b = remote(tokens_ref.at[rng_b], xbuf.at[z, rng_ob], s_ybs.at[0], s_ybr.at[0], across)
    own_b.start()

    def both(make, act):
        pl.when(z < last)(lambda: act(make(z, 1)))
        pl.when(z > 0)(lambda: act(make(planes, -1)))

    first1 = lambda slot, step: hop1(z, slot, step, tokens_ref.at[rng_a])
    first2 = lambda slot, step: hop2(z, slot, step)
    both(first1, lambda c: c.start())
    own_a = cross_a(z, tokens_ref.at[rng_a])
    own_a.start()

    def share_copy(k):
        to = lax.rem(me + k, members)
        return remote(shares_ref.at[to], sbuf.at[me], s_ssend.at[k], s_srecv.at[k], {"ep": to})

    for k in range(1, members):
        share_copy(k).start()
    sbuf[me] = shares_ref[me]
    weights = [remote(wg_hbm.at[0], wg.at[1], s_wsend.at[0], s_wrecv.at[0], twin),
               remote(wu_hbm.at[0], wu.at[1], s_wsend.at[1], s_wrecv.at[1], twin),
               remote(wd_hbm.at[0], wd.at[pl.ds(hidden, hidden)], s_wsend.at[2], s_wrecv.at[2], twin)]
    for copy in weights:
        copy.start()

    loads[0].wait()
    own_b.wait_recv()
    both(first2, lambda c: c.start())

    def order(s):
        if planes == 2:
            near = s
        else:
            near = jnp.where(end, s, jnp.where(s == 0, 1, jnp.where(s == 1, 0, s)))
        return jnp.where(low, near, last - near)

    def forward(p, act1, act2):
        pl.when((p < z) & (z < last))(lambda: act1(hop1(p, p, 1, xbuf.at[p, rng_a]), hop2(p, p, 1)))
        pl.when((p > z) & (z > 0))(lambda: act1(hop1(p, p, -1, xbuf.at[p, rng_a]), hop2(p, p, -1)))

    def relay(s):
        p = order(s)
        hop1(p, p, 0, xbuf.at[p, rng_a]).wait_recv()
        forward(p, lambda a, b: a.start(), None)
        cross_a(p, xbuf.at[p, rng_a]).start()

        @pl.when(inner)
        def _():
            hop2(p, p, 0).wait_recv()
            forward(p, lambda a, b: b.start(), None)

    def column(src, e):
        line = sbuf[src, pl.ds(e, 1), :]
        diag = lax.broadcasted_iota(jnp.int32, (rows, rows), 0) == lax.broadcasted_iota(jnp.int32, (rows, rows), 1)
        return jnp.sum(jnp.where(diag, jnp.broadcast_to(line, (rows, rows)), 0.0), axis=1, keepdims=True)

    def arrived(p):
        cross_a(p, xbuf.at[p, rng_a]).wait_recv()
        for e in range(2):
            mine = jnp.broadcast_to(column(p * 2 + y, e), (rows, 128))
            other = jnp.broadcast_to(column(p * 2 + 1 - y, e), (rows, 128))
            scale[e, rng_a, :] = mine[:row_a]
            scale[e, rng_oa, :] = other[:row_a]
            scale[e, rng_mb, :] = mine[row_a:]
            scale[e, rng_ob, :] = other[row_a:]

    tile = 256

    def make_hidden(p, e, part):
        @pl.loop(0, hidden // tile)
        def _(t):
            cols = pl.ds(pl.multiple_of(t * tile, tile), tile)
            x = xbuf[p, part, :]
            g = jnp.dot(x, wg[e, :, cols], preferred_element_type=jnp.float32)
            u = jnp.dot(x, wu[e, :, cols], preferred_element_type=jnp.float32)
            h = g / (1.0 + jnp.exp(-g)) * u * scale[e, part, pl.ds(0, 1)]
            hid[part, pl.ds(pl.multiple_of(e * hidden + t * tile, tile), tile)] = h.astype(jnp.bfloat16)

    def part_y(p, n):
        return remote(ysend.at[p, n], yrecv.at[p, n], s_pys.at[p, n], s_pyr.at[p, n], across)

    def part_z(p, n, step, b):
        slot = jnp.where((step < 0) & (z + step == p), planes, p)
        src, dst, send, recv = (zsend_b, zrecv_b, s_pzs_b, s_pzr_b) if b else (zsend_a, zrecv_a, s_pzs_a, s_pzr_a)
        return remote(src.at[p, n], dst.at[slot, n], send.at[p, n], recv.at[slot, n], {"ep": (z + step) * 2 + y})

    def from_z(slot, n, b):
        src, dst, send, recv = (zsend_b, zrecv_b, s_pzs_b, s_pzr_b) if b else (zsend_a, zrecv_a, s_pzs_a, s_pzr_a)
        remote(src.at[0, n], dst.at[slot, n], send.at[0, n], recv.at[slot, n], across).wait_recv()
        own_p = jnp.where(slot == planes, z, slot)
        part = own_bb if b else rng_a
        own[own_p, n, part, :] = own[own_p, n, part, :] + dst[slot, n].astype(jnp.float32)

    def toward(p, act):
        pl.when(p < z)(lambda: act(-1))
        pl.when(p > z)(lambda: act(1))

    def add_y(p, n):
        part_y(p, n).wait_recv()
        own[p, n, pl.ds(0, row_a), :] = own[p, n, pl.ds(0, row_a), :] + yrecv[p, n].astype(jnp.float32)

    def make_down(p, b):
        part = rng_bb if b else rng_aa

        @pl.loop(0, chunks)
        def _(n):
            acc = jnp.dot(hid[part, :], wd[:, pl.ds(pl.multiple_of(n * wide, wide), wide)], preferred_element_type=jnp.float32)
            if b:
                own[p, n, own_bb, :] = acc

                @pl.when(end)
                def _():
                    zsend_b[p, n] = acc.astype(jnp.bfloat16)
                    toward(p, lambda step: part_z(p, n, step, True).start())
            else:
                ysend[p, n] = acc[row_a:].astype(jnp.bfloat16)
                part_y(p, n).start()
                own[p, n, rng_a, :] = acc[:row_a]

    def reduce_a(p, n):
        add_y(p, n)
        pl.when(inner)(lambda: from_z(p, n, False))
        zsend_a[p, n] = own[p, n, rng_a, :].astype(jnp.bfloat16)
        toward(p, lambda step: part_z(p, n, step, False).start())

    def reduce_b(p, n):
        from_z(p, n, True)
        zsend_b[p, n] = own[p, n, own_bb, :].astype(jnp.bfloat16)
        toward(p, lambda step: part_z(p, n, step, True).start())

    for copy in loads[1:]:
        copy.wait()
    for k in range(1, members):
        share_copy(k).wait_recv()
    arrived(z)
    make_hidden(z, 0, pl.ds(0, 2 * rows))
    relay(1)
    pl.when(inner)(lambda: relay(2))
    for copy in weights:
        copy.wait_recv()
    make_hidden(z, 1, pl.ds(0, 2 * rows))
    make_down(z, False)
    make_down(z, True)

    @pl.loop(1, planes)
    def _(s):
        p = order(s)
        pl.when((s == 2) | ((s == 3) & end))(lambda: relay(jnp.where(inner, s + 1, s)))
        arrived(p)
        pl.loop(0, 2)(lambda e: make_hidden(p, e, rng_aa))
        make_down(p, False)
        pl.when(end)(lambda: hop2(p, p, 0).wait_recv())
        pl.loop(0, 2)(lambda e: make_hidden(p, e, rng_bb))
        make_down(p, True)

        @pl.when(end)
        def _():
            pl.loop(0, chunks)(lambda n: reduce_a(p, n))

    @pl.when(inner)
    def _():
        near = jnp.where(low, 0, last)
        pl.loop(0, chunks)(lambda n: reduce_b(last - z, n))
        pl.loop(0, chunks)(lambda n: reduce_a(last - z, n))

        @pl.loop(0, chunks)
        def _(n):
            reduce_b(last - near, n)
            reduce_b(near, n)

        @pl.loop(0, chunks)
        def _(n):
            reduce_a(last - near, n)
            reduce_a(near, n)

    def part_b(n):
        return remote(bsend.at[n], brecv.at[n], s_pbs.at[n], s_pbr.at[n], across)

    @pl.loop(0, chunks)
    def _(n):
        pl.when(z > 0)(lambda: from_z(z, n, True))
        pl.when(z < last)(lambda: from_z(planes, n, True))
        bsend[n] = own[z, n, pl.ds(row_a + row_b, row_b), :].astype(jnp.bfloat16)
        part_b(n).start()

    for n in range(chunks):
        cols = pl.ds(n * wide, wide)
        add_y(z, n)
        pl.when(z > 0)(lambda: from_z(z, n, False))
        pl.when(z < last)(lambda: from_z(planes, n, False))
        out_ref[rng_a, cols] = own[z, n, rng_a, :].astype(jnp.bfloat16)

    for n in range(chunks):
        part_b(n).wait_recv()
        cols = pl.ds(n * wide, wide)
        out_ref[rng_b, cols] = (own[z, n, rng_b, :] + brecv[n].astype(jnp.float32)).astype(jnp.bfloat16)

    own_b.wait_send()
    both(first1, lambda c: c.wait_send())
    both(first2, lambda c: c.wait_send())
    for k in range(1, members):
        share_copy(k).wait_send()
    for copy in weights:
        copy.wait_send()

    def both_sent(a, b):
        a.wait_send()
        b.wait_send()

    @pl.loop(0, planes)
    def _(p):
        cross_a(p, xbuf.at[p, rng_a]).wait_send()
        forward(p, both_sent, None)

        @pl.loop(0, chunks)
        def _(n):
            part_y(p, n).wait_send()
            toward(p, lambda step: both_sent(part_z(p, n, step, False), part_z(p, n, step, True)))

    for n in range(chunks):
        part_b(n).wait_send()


def fused(tokens, routes, gates, w_gate, w_up, w_down):
    rows, width = tokens.shape
    hidden = w_gate.shape[2]
    members = lax.axis_size("ep")
    planes = members // 2
    row_b = rows * B_SHARE // 8
    row_a = rows - row_b
    kept = row_a + 2 * row_b
    chunks = 2
    wide = width // chunks
    core = lax.axis_index("grp")
    ids = lax.rem(core + jnp.arange(8, dtype=jnp.int32), 2)[None, :] * members + jnp.arange(members, dtype=jnp.int32)[:, None]
    shares = jnp.sum(jnp.where(routes.T[:, None, None, :] == ids[None, :, :, None], gates.T[:, None, None, :], 0.0), axis=0)
    bf, dma = jnp.bfloat16, pltpu.SemaphoreType.DMA
    flops = 2 * members * rows * width * hidden * 6
    return pl.pallas_call(
        mixing_kernel,
        out_shape=jax.ShapeDtypeStruct((rows, width), bf),
        in_specs=[pl.BlockSpec(memory_space=pltpu.VMEM)] * 2 + [pl.BlockSpec(memory_space=pl.ANY)] * 3,
        out_specs=pl.BlockSpec(memory_space=pltpu.VMEM),
        scratch_shapes=[
            pltpu.VMEM((planes, 2 * rows, width), bf),
            pltpu.VMEM((members, 8, rows), jnp.float32),
            pltpu.VMEM((2, width, hidden), bf),
            pltpu.VMEM((2, width, hidden), bf),
            pltpu.VMEM((2 * hidden, width), bf),
            pltpu.VMEM((2 * rows, 2 * hidden), bf),
            pltpu.VMEM((2, 2 * rows, 128), jnp.float32),
            pltpu.VMEM((planes, chunks, kept, wide), jnp.float32),
            pltpu.VMEM((planes, chunks, row_a, wide), bf),
            pltpu.VMEM((planes, chunks, row_a, wide), bf),
            pltpu.VMEM((planes, chunks, row_a, wide), bf),
            pltpu.VMEM((planes, chunks, 2 * row_b, wide), bf),
            pltpu.VMEM((planes + 1, chunks, row_a, wide), bf),
            pltpu.VMEM((planes + 1, chunks, 2 * row_b, wide), bf),
            pltpu.VMEM((chunks, row_b, wide), bf),
            pltpu.VMEM((chunks, row_b, wide), bf),
            dma((5,)), dma((3,)), dma((3,)), dma((members,)), dma((members,)),
            dma((planes + 1,)), dma((planes + 1,)), dma((planes,)), dma((planes,)),
            dma((planes,)), dma((planes,)), dma((1,)), dma((1,)),
            dma((planes, chunks)), dma((planes, chunks)), dma((planes, chunks)), dma((planes + 1, chunks)),
            dma((planes, chunks)), dma((planes + 1, chunks)),
            dma((chunks,)), dma((chunks,)),
        ],
        compiler_params=pltpu.CompilerParams(collective_id=0, has_side_effects=True, vmem_limit_bytes=60 * 1024 * 1024),
        cost_estimate=pl.CostEstimate(flops=flops, bytes_accessed=20 * 1024 * 1024, transcendentals=0),
    )(tokens, shares, w_gate, w_up, w_down)


def solution(mesh):
    groups, members = mesh.shape["grp"], mesh.shape["ep"]

    def local(tokens, routes, gates, w_gate, w_up, w_down):
        dense = groups == 2 and members == 8 and routes.shape[1] * 3 >= groups * members
        body = fused if dense else routed
        return body(tokens, routes, gates, w_gate, w_up, w_down)

    return jax.shard_map(
        local,
        mesh=mesh,
        in_specs=(
            P(("rep", "grp", "ep"), None),
            P(("rep", "grp", "ep"), None),
            P(("rep", "grp", "ep"), None),
            P(("grp", "ep"), None, None),
            P(("grp", "ep"), None, None),
            P(("grp", "ep"), None, None),
        ),
        out_specs=P(("rep", "grp", "ep"), None),
        check_vma=False,
    )
```

```python
import jax
import jax.numpy as jnp
from jax import lax
from jax.experimental import pallas as pl
from jax.experimental.pallas import tpu as pltpu
from jax.sharding import PartitionSpec as P

B_SHARE = 4


def expert_rows(rows, w_gate, w_up, w_down):
    gate_act = jnp.dot(rows, w_gate[0], preferred_element_type=jnp.float32)
    up_act = jnp.dot(rows, w_up[0], preferred_element_type=jnp.float32)
    hidden = (jax.nn.silu(gate_act) * up_act).astype(jnp.bfloat16)
    return jnp.dot(hidden, w_down[0], preferred_element_type=jnp.float32).astype(jnp.bfloat16)


def routed(tokens, routes, gates, w_gate, w_up, w_down):
    tok_rows, width = tokens.shape
    top = routes.shape[1]
    groups = lax.axis_size("grp")
    members = lax.axis_size("ep")
    experts = groups * members
    capacity = tok_rows * top * 3 // (2 * experts)
    flat_ids = routes.reshape(-1)
    onehot = (flat_ids[:, None] == jnp.arange(experts, dtype=jnp.int32)[None, :]).astype(jnp.int32)
    ranks = jnp.cumsum(onehot, axis=0) - 1
    slot = jnp.sum(ranks * onehot, axis=1)
    position = flat_ids * capacity + slot
    token_idx = jnp.arange(tok_rows * top, dtype=jnp.int32) // top
    send = jnp.zeros((experts * capacity, width), jnp.bfloat16).at[position].set(tokens[token_idx])
    sectioned = send.reshape(groups, members, capacity, width)
    arrived = lax.all_to_all(
        lax.all_to_all(sectioned, "grp", split_axis=0, concat_axis=0, tiled=True),
        "ep",
        split_axis=1,
        concat_axis=1,
        tiled=True,
    )
    results = expert_rows(arrived.reshape(-1, width), w_gate, w_up, w_down)
    results = results.reshape(groups, members, capacity, width)
    back = lax.all_to_all(
        lax.all_to_all(results, "grp", split_axis=0, concat_axis=0, tiled=True),
        "ep",
        split_axis=1,
        concat_axis=1,
        tiled=True,
    )
    picked = back.reshape(experts * capacity, width)[position].astype(jnp.float32)
    picked = picked.reshape(tok_rows, top, width)
    mixed = jnp.sum(picked * gates[:, :, None], axis=1)
    return mixed.astype(jnp.bfloat16)


def mixing_kernel(tokens_ref, shares_ref, wg_hbm, wu_hbm, wd_hbm, out_ref,
                  xbuf, sbuf, wg, wu, wd, hid, scale, own, ysend, yrecv, zsend_a, zsend_b, zrecv_a, zrecv_b, bsend, brecv,
                  s_load, s_wsend, s_wrecv, s_ssend, s_srecv,
                  s_zs1, s_zs2, s_zr1, s_zr2, s_yas, s_yar, s_ybs, s_ybr,
                  s_pys, s_pyr, s_pzs_a, s_pzr_a, s_pzs_b, s_pzr_b, s_pbs, s_pbr):
    rows = tokens_ref.shape[0]
    row_b = brecv.shape[1]
    row_a = rows - row_b
    hidden = wg.shape[2]
    chunks, _, wide = bsend.shape
    planes = xbuf.shape[0]
    last = planes - 1
    members = 2 * planes
    me = lax.axis_index("ep")
    core = lax.axis_index("grp")
    z, y = me // 2, me % 2
    twin = {"grp": 1 - core}
    across = {"ep": z * 2 + (1 - y)}
    end = (z == 0) | (z == last)
    inner = jnp.logical_not(end)
    low = z < planes // 2

    def remote(src, dst, send, recv, to):
        return pltpu.make_async_remote_copy(src_ref=src, dst_ref=dst, send_sem=send, recv_sem=recv, device_id=to,
                                            device_id_type=pl.DeviceIdType.MESH)

    barrier = pltpu.get_barrier_semaphore()
    pl.semaphore_signal(barrier, inc=1, device_id=twin, device_id_type=pl.DeviceIdType.MESH)
    for k in range(1, members):
        pl.semaphore_signal(barrier, inc=1, device_id={"ep": lax.rem(me + k, members)}, device_id_type=pl.DeviceIdType.MESH)

    rng_a, rng_b = pl.ds(0, row_a), pl.ds(row_a, row_b)
    rng_oa, rng_mb = pl.ds(row_a, row_a), pl.ds(2 * row_a, row_b)
    rng_ob, rng_bb = pl.ds(2 * row_a + row_b, row_b), pl.ds(2 * row_a, 2 * row_b)
    rng_aa = pl.ds(0, 2 * row_a)
    own_bb = pl.ds(row_a, 2 * row_b)

    loads = [pltpu.make_async_copy(tokens_ref.at[rng_b], xbuf.at[z, rng_mb], s_load.at[0]),
             pltpu.make_async_copy(tokens_ref.at[rng_a], xbuf.at[z, rng_a], s_load.at[4]),
             pltpu.make_async_copy(wg_hbm.at[0], wg.at[0], s_load.at[1]),
             pltpu.make_async_copy(wu_hbm.at[0], wu.at[0], s_load.at[2]),
             pltpu.make_async_copy(wd_hbm.at[0], wd.at[pl.ds(0, hidden)], s_load.at[3])]
    for copy in loads:
        copy.start()
    pl.semaphore_wait(barrier, members)

    def hop1(p, slot, step, src):
        return remote(src, xbuf.at[p, rng_a], s_zs1.at[slot], s_zr1.at[p], {"ep": (z + step) * 2 + y})

    def hop2(p, slot, step):
        return remote(xbuf.at[p, rng_bb], xbuf.at[p, rng_bb], s_zs2.at[slot], s_zr2.at[p], {"ep": (z + step) * 2 + y})

    def cross_a(p, src):
        return remote(src, xbuf.at[p, rng_oa], s_yas.at[p], s_yar.at[p], across)

    own_b = remote(tokens_ref.at[rng_b], xbuf.at[z, rng_ob], s_ybs.at[0], s_ybr.at[0], across)
    own_b.start()

    def both(make, act):
        pl.when(z < last)(lambda: act(make(z, 1)))
        pl.when(z > 0)(lambda: act(make(planes, -1)))

    first1 = lambda slot, step: hop1(z, slot, step, tokens_ref.at[rng_a])
    first2 = lambda slot, step: hop2(z, slot, step)
    both(first1, lambda c: c.start())
    own_a = cross_a(z, tokens_ref.at[rng_a])
    own_a.start()

    def share_copy(k):
        to = lax.rem(me + k, members)
        return remote(shares_ref.at[to], sbuf.at[me], s_ssend.at[k], s_srecv.at[k], {"ep": to})

    for k in range(1, members):
        share_copy(k).start()
    sbuf[me] = shares_ref[me]
    weights = [remote(wg_hbm.at[0], wg.at[1], s_wsend.at[0], s_wrecv.at[0], twin),
               remote(wu_hbm.at[0], wu.at[1], s_wsend.at[1], s_wrecv.at[1], twin),
               remote(wd_hbm.at[0], wd.at[pl.ds(hidden, hidden)], s_wsend.at[2], s_wrecv.at[2], twin)]
    for copy in weights:
        copy.start()

    loads[0].wait()
    own_b.wait_recv()
    both(first2, lambda c: c.start())

    def order(s):
        if planes == 2:
            near = s
        else:
            near = jnp.where(end, s, jnp.where(s == 0, 1, jnp.where(s == 1, 0, s)))
        return jnp.where(low, near, last - near)

    def forward(p, act1, act2):
        pl.when((p < z) & (z < last))(lambda: act1(hop1(p, p, 1, xbuf.at[p, rng_a]), hop2(p, p, 1)))
        pl.when((p > z) & (z > 0))(lambda: act1(hop1(p, p, -1, xbuf.at[p, rng_a]), hop2(p, p, -1)))

    def relay(s):
        p = order(s)
        hop1(p, p, 0, xbuf.at[p, rng_a]).wait_recv()
        forward(p, lambda a, b: a.start(), None)
        cross_a(p, xbuf.at[p, rng_a]).start()

        @pl.when(inner)
        def _():
            hop2(p, p, 0).wait_recv()
            forward(p, lambda a, b: b.start(), None)

    def column(src, e):
        line = sbuf[src, pl.ds(e, 1), :]
        diag = lax.broadcasted_iota(jnp.int32, (rows, rows), 0) == lax.broadcasted_iota(jnp.int32, (rows, rows), 1)
        return jnp.sum(jnp.where(diag, jnp.broadcast_to(line, (rows, rows)), 0.0), axis=1, keepdims=True)

    def arrived(p):
        cross_a(p, xbuf.at[p, rng_a]).wait_recv()
        for e in range(2):
            mine = jnp.broadcast_to(column(p * 2 + y, e), (rows, 128))
            other = jnp.broadcast_to(column(p * 2 + 1 - y, e), (rows, 128))
            scale[e, rng_a, :] = mine[:row_a]
            scale[e, rng_oa, :] = other[:row_a]
            scale[e, rng_mb, :] = mine[row_a:]
            scale[e, rng_ob, :] = other[row_a:]

    tile = 768

    def make_hidden(p, e, part):
        @pl.loop(0, hidden // tile)
        def _(t):
            cols = pl.ds(pl.multiple_of(t * tile, tile), tile)
            x = xbuf[p, part, :]
            g = jnp.dot(x, wg[e, :, cols], preferred_element_type=jnp.float32)
            u = jnp.dot(x, wu[e, :, cols], preferred_element_type=jnp.float32)
            h = g / (1.0 + jnp.exp(-g)) * u * scale[e, part, pl.ds(0, 1)]
            hid[part, pl.ds(pl.multiple_of(e * hidden + t * tile, tile), tile)] = h.astype(jnp.bfloat16)

    def part_y(p, n):
        return remote(ysend.at[p, n], yrecv.at[p, n], s_pys.at[p, n], s_pyr.at[p, n], across)

    def part_z(p, n, step, b):
        slot = jnp.where((step < 0) & (z + step == p), planes, p)
        src, dst, send, recv = (zsend_b, zrecv_b, s_pzs_b, s_pzr_b) if b else (zsend_a, zrecv_a, s_pzs_a, s_pzr_a)
        return remote(src.at[p, n], dst.at[slot, n], send.at[p, n], recv.at[slot, n], {"ep": (z + step) * 2 + y})

    def from_z(slot, n, b):
        src, dst, send, recv = (zsend_b, zrecv_b, s_pzs_b, s_pzr_b) if b else (zsend_a, zrecv_a, s_pzs_a, s_pzr_a)
        remote(src.at[0, n], dst.at[slot, n], send.at[0, n], recv.at[slot, n], across).wait_recv()
        own_p = jnp.where(slot == planes, z, slot)
        part = own_bb if b else rng_a
        own[own_p, n, part, :] = own[own_p, n, part, :] + dst[slot, n].astype(jnp.float32)

    def toward(p, act):
        pl.when(p < z)(lambda: act(-1))
        pl.when(p > z)(lambda: act(1))

    def add_y(p, n):
        part_y(p, n).wait_recv()
        own[p, n, pl.ds(0, row_a), :] = own[p, n, pl.ds(0, row_a), :] + yrecv[p, n].astype(jnp.float32)

    def make_down(p, b):
        part = rng_bb if b else rng_aa

        @pl.loop(0, chunks)
        def _(n):
            acc = jnp.dot(hid[part, :], wd[:, pl.ds(pl.multiple_of(n * wide, wide), wide)], preferred_element_type=jnp.float32)
            if b:
                own[p, n, own_bb, :] = acc

                @pl.when(end)
                def _():
                    zsend_b[p, n] = acc.astype(jnp.bfloat16)
                    toward(p, lambda step: part_z(p, n, step, True).start())
            else:
                ysend[p, n] = acc[row_a:].astype(jnp.bfloat16)
                part_y(p, n).start()
                own[p, n, rng_a, :] = acc[:row_a]

    def reduce_a(p, n):
        add_y(p, n)
        pl.when(inner)(lambda: from_z(p, n, False))
        zsend_a[p, n] = own[p, n, rng_a, :].astype(jnp.bfloat16)
        toward(p, lambda step: part_z(p, n, step, False).start())

    def reduce_b(p, n):
        from_z(p, n, True)
        zsend_b[p, n] = own[p, n, own_bb, :].astype(jnp.bfloat16)
        toward(p, lambda step: part_z(p, n, step, True).start())

    for copy in loads[1:]:
        copy.wait()
    for k in range(1, members):
        share_copy(k).wait_recv()
    arrived(z)
    make_hidden(z, 0, pl.ds(0, 2 * rows))
    relay(1)
    pl.when(inner)(lambda: relay(2))
    for copy in weights:
        copy.wait_recv()
    make_hidden(z, 1, pl.ds(0, 2 * rows))
    make_down(z, False)
    make_down(z, True)

    @pl.loop(1, planes)
    def _(s):
        p = order(s)
        pl.when((s == 2) | ((s == 3) & end))(lambda: relay(jnp.where(inner, s + 1, s)))
        arrived(p)
        pl.loop(0, 2)(lambda e: make_hidden(p, e, rng_aa))
        make_down(p, False)
        pl.when(end)(lambda: hop2(p, p, 0).wait_recv())
        pl.loop(0, 2)(lambda e: make_hidden(p, e, rng_bb))
        make_down(p, True)

        @pl.when(end)
        def _():
            pl.loop(0, chunks)(lambda n: reduce_a(p, n))

    @pl.when(inner)
    def _():
        near = jnp.where(low, 0, last)
        pl.loop(0, chunks)(lambda n: reduce_b(last - z, n))
        pl.loop(0, chunks)(lambda n: reduce_a(last - z, n))

        @pl.loop(0, chunks)
        def _(n):
            reduce_b(last - near, n)
            reduce_b(near, n)

        @pl.loop(0, chunks)
        def _(n):
            reduce_a(last - near, n)
            reduce_a(near, n)

    def part_b(n):
        return remote(bsend.at[n], brecv.at[n], s_pbs.at[n], s_pbr.at[n], across)

    @pl.loop(0, chunks)
    def _(n):
        pl.when(z > 0)(lambda: from_z(z, n, True))
        pl.when(z < last)(lambda: from_z(planes, n, True))
        bsend[n] = own[z, n, pl.ds(row_a + row_b, row_b), :].astype(jnp.bfloat16)
        part_b(n).start()

    for n in range(chunks):
        cols = pl.ds(n * wide, wide)
        add_y(z, n)
        pl.when(z > 0)(lambda: from_z(z, n, False))
        pl.when(z < last)(lambda: from_z(planes, n, False))
        out_ref[rng_a, cols] = own[z, n, rng_a, :].astype(jnp.bfloat16)

    for n in range(chunks):
        part_b(n).wait_recv()
        cols = pl.ds(n * wide, wide)
        out_ref[rng_b, cols] = (own[z, n, rng_b, :] + brecv[n].astype(jnp.float32)).astype(jnp.bfloat16)

    own_b.wait_send()
    both(first1, lambda c: c.wait_send())
    both(first2, lambda c: c.wait_send())
    for k in range(1, members):
        share_copy(k).wait_send()
    for copy in weights:
        copy.wait_send()

    def both_sent(a, b):
        a.wait_send()
        b.wait_send()

    @pl.loop(0, planes)
    def _(p):
        cross_a(p, xbuf.at[p, rng_a]).wait_send()
        forward(p, both_sent, None)

        @pl.loop(0, chunks)
        def _(n):
            part_y(p, n).wait_send()
            toward(p, lambda step: both_sent(part_z(p, n, step, False), part_z(p, n, step, True)))

    for n in range(chunks):
        part_b(n).wait_send()


def fused(tokens, routes, gates, w_gate, w_up, w_down):
    rows, width = tokens.shape
    hidden = w_gate.shape[2]
    members = lax.axis_size("ep")
    planes = members // 2
    row_b = rows * B_SHARE // 8
    row_a = rows - row_b
    kept = row_a + 2 * row_b
    chunks = 2
    wide = width // chunks
    core = lax.axis_index("grp")
    ids = lax.rem(core + jnp.arange(8, dtype=jnp.int32), 2)[None, :] * members + jnp.arange(members, dtype=jnp.int32)[:, None]
    shares = jnp.sum(jnp.where(routes.T[:, None, None, :] == ids[None, :, :, None], gates.T[:, None, None, :], 0.0), axis=0)
    bf, dma = jnp.bfloat16, pltpu.SemaphoreType.DMA
    flops = 2 * members * rows * width * hidden * 6
    return pl.pallas_call(
        mixing_kernel,
        out_shape=jax.ShapeDtypeStruct((rows, width), bf),
        in_specs=[pl.BlockSpec(memory_space=pltpu.VMEM)] * 2 + [pl.BlockSpec(memory_space=pl.ANY)] * 3,
        out_specs=pl.BlockSpec(memory_space=pltpu.VMEM),
        scratch_shapes=[
            pltpu.VMEM((planes, 2 * rows, width), bf),
            pltpu.VMEM((members, 8, rows), jnp.float32),
            pltpu.VMEM((2, width, hidden), bf),
            pltpu.VMEM((2, width, hidden), bf),
            pltpu.VMEM((2 * hidden, width), bf),
            pltpu.VMEM((2 * rows, 2 * hidden), bf),
            pltpu.VMEM((2, 2 * rows, 128), jnp.float32),
            pltpu.VMEM((planes, chunks, kept, wide), jnp.float32),
            pltpu.VMEM((planes, chunks, row_a, wide), bf),
            pltpu.VMEM((planes, chunks, row_a, wide), bf),
            pltpu.VMEM((planes, chunks, row_a, wide), bf),
            pltpu.VMEM((planes, chunks, 2 * row_b, wide), bf),
            pltpu.VMEM((planes + 1, chunks, row_a, wide), bf),
            pltpu.VMEM((planes + 1, chunks, 2 * row_b, wide), bf),
            pltpu.VMEM((chunks, row_b, wide), bf),
            pltpu.VMEM((chunks, row_b, wide), bf),
            dma((5,)), dma((3,)), dma((3,)), dma((members,)), dma((members,)),
            dma((planes + 1,)), dma((planes + 1,)), dma((planes,)), dma((planes,)),
            dma((planes,)), dma((planes,)), dma((1,)), dma((1,)),
            dma((planes, chunks)), dma((planes, chunks)), dma((planes, chunks)), dma((planes + 1, chunks)),
            dma((planes, chunks)), dma((planes + 1, chunks)),
            dma((chunks,)), dma((chunks,)),
        ],
        compiler_params=pltpu.CompilerParams(collective_id=0, has_side_effects=True, vmem_limit_bytes=60 * 1024 * 1024),
        cost_estimate=pl.CostEstimate(flops=flops, bytes_accessed=20 * 1024 * 1024, transcendentals=0),
    )(tokens, shares, w_gate, w_up, w_down)


def solution(mesh):
    groups, members = mesh.shape["grp"], mesh.shape["ep"]

    def local(tokens, routes, gates, w_gate, w_up, w_down):
        dense = groups == 2 and members == 8 and routes.shape[1] * 3 >= groups * members
        body = fused if dense else routed
        return body(tokens, routes, gates, w_gate, w_up, w_down)

    return jax.shard_map(
        local,
        mesh=mesh,
        in_specs=(
            P(("rep", "grp", "ep"), None),
            P(("rep", "grp", "ep"), None),
            P(("rep", "grp", "ep"), None),
            P(("grp", "ep"), None, None),
            P(("grp", "ep"), None, None),
            P(("grp", "ep"), None, None),
        ),
        out_specs=P(("rep", "grp", "ep"), None),
        check_vma=False,
    )
```
